512 devices in a mesh: blk: 32 (over x_hi, z, core), split: 16 (over x_lo, y).
Axes of the slice: x: 4 (x_hi: 2, x_lo: 2; x = x_hi * 2 + x_lo), y: 8, z: 8, core: 2. Of those that a mesh axis runs over, the one named last changes fastest.
Arguments:
- orbitals: float32 [16384, 512], P('blk'), may hold values from -6 to 6
- kernel: float32 [16384, 16, 1024], P('blk', 'split'), as said below
Outputs:
- exchange_out: float32 [16384, 512], P(('blk', 'split'))
The draws below stay inside these ranges and needn't reach their ends.
Inputs may be any that keep to these rules, and one draw needn't show every extreme that they name: Z built from kernel as in the first step is a symmetric matrix.
All inputs are finite; a program needn't handle non-finite values.
Results may differ from the reference program's by a relative error of at most 0.00013.
Values sent between devices are 32-bit elements; how exact they have to be, the bound alone decides.
A program may use at most 64 MiB of HBM per device.

```python
import jax
import jax.numpy as jnp
from jax import lax

NORB = 512
PB = 512
NPTS = 16384
SHARE = 32
N_BLK = 32
N_SPLIT = 16


def draw_kernel(key, part):
    total = NPTS
    first = jax.random.normal(jax.random.fold_in(key, 11), (total, total), jnp.float32)
    sym = (first + first.T) * 0.5 ** 0.5
    sym = sym / jnp.sqrt(jnp.float32(total * NORB))
    sym = sym.reshape(total, N_BLK, N_SPLIT, SHARE)
    sym = jnp.transpose(sym, (0, 2, 1, 3))
    return sym.reshape(total, N_SPLIT, N_BLK * SHARE)


def level_of(stream_key, shape, cuts, low, top_value):
    level, own = 1.0, jax.random.fold_in(stream_key, 6)
    for axis_at, shards_of in cuts:
        heights = jnp.exp(jax.random.uniform(jax.random.fold_in(own, axis_at), (shards_of,), jnp.float32, low / len(cuts), top_value / len(cuts)))
        level = level * jnp.repeat(heights, shape[axis_at] // shards_of).reshape([-1 if axis == axis_at else 1 for axis in range(len(shape))])
    return level


def normal_values(own_key, shape, spread, limit, split=(), kind=jnp.bfloat16):
    gain = level_of(own_key, shape, split, -0.22, 0.18) if split else 1.0
    array = jax.random.normal(own_key, shape, jnp.float32) * spread * gain
    return jnp.minimum(jnp.maximum(array, -limit), limit).astype(kind)


def setup_inputs(seed: int = 0) -> dict:
    keys = jax.random.split(jax.random.key(seed), 3)
    return {
        "orbitals": normal_values(keys[0], (NPTS, NORB), 1.0, 6.0, ((0, 32),), jnp.float32),
        "kernel": draw_kernel(jax.random.fold_in(keys[2], 71), 0),
    }


def reference(orbitals, kernel):
    blocks_orb = orbitals.reshape(N_BLK, PB, NORB)
    blocks_ker = kernel.reshape(N_BLK, PB, N_SPLIT, N_BLK, SHARE)

    def one_block(pieces):
        rows_orb, rows_ker = pieces
        z_rows = jnp.transpose(rows_ker, (0, 2, 1, 3)).reshape(PB, NPTS)
        density = jnp.dot(rows_orb, orbitals.T, precision=lax.Precision.HIGHEST, preferred_element_type=jnp.float32)
        weighted = z_rows * density
        return jnp.dot(weighted, orbitals, precision=lax.Precision.HIGHEST, preferred_element_type=jnp.float32)

    result = lax.map(one_block, (blocks_orb, blocks_ker))
    return result.reshape(NPTS, NORB)
```

```python
import functools

import jax
import jax.numpy as jnp
from jax import lax
from jax.experimental import pallas as pl
from jax.experimental.pallas import tpu as pltpu
from jax.sharding import PartitionSpec as P

MESH = pl.DeviceIdType.MESH
F32 = jnp.float32
BF16 = jnp.bfloat16

NX, NZ, NC = 2, 8, 2
NXL, NY = 2, 8
SH = 32
NORB = 512
PB = 512

GATHER = [("gx",)] + [
    ("gz", plane, sign, hop)
    for plane in (0, 1)
    for sign in (1, -1)
    for hop in range(1, 5)
    if hop < 4 or sign == (1 if plane == 0 else -1)
]
CORE = [("gc", plane, off) for plane in (0, 1) for off in range(NZ)]
REDUCE = [
    ("r", plane, sign, dist)
    for plane in (0, 1)
    for sign in (1, -1)
    for dist in range(1, 5)
    if dist < 4 or sign == (1 if plane == 0 else -1)
]
SEM = {name: at for at, name in enumerate(GATHER + CORE + REDUCE + [("rx",)])}
SLOT = {name: at for at, name in enumerate(REDUCE)}


def split_bf16(value):
    high = value.astype(BF16)
    return high, (value - high.astype(F32)).astype(BF16)


def exchange(
    orb_hbm, ker_hbm, out_ref, ker, orb, gat, lhs, rhs, pair_rhs, dens, wts, part, landed, folded, ssem, rsem, lsem
):
    b = lax.axis_index("blk")
    s = lax.axis_index("split")
    xh, z, c = b // (NZ * NC), (b // NC) % NZ, b % NC
    xl, y = s // NY, s % NY

    def blk_of(plane, off):
        return ((xh + plane) % NX) * (NZ * NC) + ((z + off + NZ) % NZ) * NC + c

    x_peer = (blk_of(1, 0), s)
    core_peer = (b + 1 - 2 * c, s)
    z_peer = {sign: (blk_of(0, sign), s) for sign in (1, -1)}
    y_peer = {sign: (b, xl * NY + (y + sign + NY) % NY) for sign in (1, -1)}
    xl_peer = (b, ((xl + 1) % NXL) * NY + y)
    peers = [x_peer, core_peer, z_peer[1], z_peer[-1], y_peer[1], y_peer[-1], xl_peer]

    ker_copy = pltpu.make_async_copy(ker_hbm.at[:, 0, :], ker, lsem.at[0])
    orb_copy = pltpu.make_async_copy(orb_hbm, orb, lsem.at[1])

    def share_rows(block):
        return pl.ds(pl.multiple_of(block * SH, SH), SH)

    own_copy = pltpu.make_async_copy(orb_hbm.at[share_rows(s)], gat.at[share_rows(b)], lsem.at[2])
    own_copy.start()
    orb_copy.start()
    ker_copy.start()

    barrier = pltpu.get_barrier_semaphore()
    for peer in peers:
        pl.semaphore_signal(barrier, inc=1, device_id=peer, device_id_type=MESH)
    pl.semaphore_wait(barrier, len(peers))

    started = []

    def remote(name, src, dst, peer):
        return pltpu.make_async_remote_copy(
            src_ref=src,
            dst_ref=dst,
            send_sem=ssem.at[SEM[name]],
            recv_sem=rsem.at[SEM[name]],
            device_id=peer,
            device_id_type=MESH,
        )

    def send(name, src, dst, peer):
        copy = remote(name, src, dst, peer)
        copy.start()
        started.append(copy)

    def send_share(name, block, peer):
        rows = share_rows(block)
        send(name, gat.at[rows], gat.at[rows], peer)

    def wait_share(name, block, peer):
        rows = share_rows(block)
        remote(name, gat.at[rows], gat.at[rows], peer).wait_recv()

    def has_hop(plane, sign, hop):
        return ("gz", plane, sign, hop) in SEM

    own_copy.wait()
    send_share(("gx",), b, x_peer)
    send_share(("gz", 0, 1, 1), b, z_peer[1])
    send_share(("gz", 0, -1, 1), b, z_peer[-1])
    send_share(("gc", 0, 0), b, core_peer)
    other = blk_of(1, 0)
    wait_share(("gx",), other, x_peer)
    send_share(("gz", 1, 1, 1), other, z_peer[1])
    send_share(("gz", 1, -1, 1), other, z_peer[-1])
    send_share(("gc", 1, 0), other, core_peer)

    def gather_hop(hop):
        for plane in (0, 1):
            for sign in (1, -1):
                if not has_hop(plane, sign, hop):
                    continue
                off = -sign * hop
                block = blk_of(plane, off)
                wait_share(("gz", plane, sign, hop), block, z_peer[sign])
                if has_hop(plane, sign, hop + 1):
                    send_share(("gz", plane, sign, hop + 1), block, z_peer[sign])
                send_share(("gc", plane, off % NZ), block, core_peer)

    def wait_core(offs):
        for off in offs:
            for plane in (0, 1):
                block = blk_of(plane, off) + 1 - 2 * c
                wait_share(("gc", plane, off % NZ), block, core_peer)

    odd = z % 2
    half = NZ // 2
    pair0 = z // 2
    near = 2 * odd - 1
    pairs = [pair0, (pair0 + near + half) % half, (pair0 - near + half) % half, (pair0 + 2) % half]
    width = 2 * NC * SH

    def batch(pair, first):
        for plane in (0, 1):
            rows = pl.ds(pl.multiple_of(plane * (NZ * NC * SH) + pair * width, width), width)
            high, low = split_bf16(gat[rows, :])
            at = pl.ds(plane * width, width)
            rhs[at, pl.ds(0, NORB)] = high
            rhs[at, pl.ds(NORB, NORB)] = high
            rhs[at, pl.ds(2 * NORB, NORB)] = low
            pair_rhs[pl.ds(plane * width, width), :] = high
            pair_rhs[pl.ds((NX + plane) * width, width), :] = high
            pair_rhs[pl.ds((2 * NX + plane) * width, width), :] = low
        dens[...] = lax.dot_general(
            lhs[...], rhs[...], (((1,), (1,)), ((), ())), preferred_element_type=F32
        )
        for plane in (0, 1):
            cols = pl.ds(pl.multiple_of(plane * (NZ * NC * SH) + pair * width, width), width)
            weighted = dens[:, pl.ds(plane * width, width)] * ker[:, cols]
            high, low = split_bf16(weighted)
            wts[:, pl.ds(plane * width, width)] = high
            wts[:, pl.ds((NX + plane) * width, width)] = low
            wts[:, pl.ds((2 * NX + plane) * width, width)] = high
        product = jnp.dot(wts[...], pair_rhs[...], preferred_element_type=F32)
        if first:
            part[...] = product
        else:
            part[...] += product

    orb_copy.wait()
    high, low = split_bf16(orb[...])
    lhs[:, pl.ds(0, NORB)] = high
    lhs[:, pl.ds(NORB, NORB)] = low
    lhs[:, pl.ds(2 * NORB, NORB)] = high

    gather_hop(1)
    gather_hop(2)
    ker_copy.wait()
    wait_core([0, 1, -1])
    batch(pairs[0], True)
    gather_hop(3)
    wait_core([2, -2])
    batch(pairs[1], False)
    gather_hop(4)
    wait_core([3, -3])
    batch(pairs[2], False)
    wait_core([4])
    batch(pairs[3], False)

    def target_rows(plane, off):
        share = ((xl + plane) % NXL) * NY + (y + off + NY) % NY
        return share_rows(share)

    def slot_rows(name):
        return pl.ds(SLOT[name] * SH, SH)

    def send_partial(plane, sign, dist):
        name = ("r", plane, sign, dist)
        send(name, part.at[target_rows(plane, sign * dist)], landed.at[slot_rows(name)], y_peer[sign])

    def wait_partial(plane, sign, dist):
        name = ("r", plane, sign, dist)
        remote(name, part.at[slot_rows(name)], landed.at[slot_rows(name)], y_peer[sign]).wait_recv()
        return landed[slot_rows(name), :]

    chains = [(1, -1), (1, 1), (0, 1), (0, -1)]
    longest = {chain: max(n[3] for n in REDUCE if n[1:3] == chain) for chain in chains}
    for step in range(4):
        for plane, sign in chains:
            dist = longest[plane, sign] - step
            if dist < 1:
                continue
            if step:
                rows = target_rows(plane, sign * dist)
                part[rows, :] += wait_partial(plane, sign, dist + 1)
            send_partial(plane, sign, dist)

    folded[pl.ds(0, SH), :] = (
        part[target_rows(1, 0), :] + wait_partial(1, 1, 1) + wait_partial(1, -1, 1)
    )
    send(("rx",), folded.at[pl.ds(0, SH)], folded.at[pl.ds(SH, SH)], xl_peer)
    mine = part[target_rows(0, 0), :] + wait_partial(0, 1, 1) + wait_partial(0, -1, 1)
    remote(("rx",), folded.at[pl.ds(0, SH)], folded.at[pl.ds(SH, SH)], xl_peer).wait_recv()
    out_ref[...] = mine + folded[pl.ds(SH, SH), :]

    for copy in started:
        copy.wait_send()


def per_device(orbitals, kernel):
    columns = kernel.shape[2]
    return pl.pallas_call(
        exchange,
        out_shape=jax.ShapeDtypeStruct((SH, NORB), F32),
        in_specs=[pl.BlockSpec(memory_space=pltpu.HBM)] * 2,
        out_specs=pl.BlockSpec(memory_space=pltpu.VMEM),
        scratch_shapes=[
            pltpu.VMEM((PB, columns), F32),
            pltpu.VMEM((PB, NORB), F32),
            pltpu.VMEM((columns, NORB), F32),
            pltpu.VMEM((PB, 3 * NORB), BF16),
            pltpu.VMEM((256, 3 * NORB), BF16),
            pltpu.VMEM((3 * 256, NORB), BF16),
            pltpu.VMEM((PB, 256), F32),
            pltpu.VMEM((PB, 3 * 256), BF16),
            pltpu.VMEM((PB, NORB), F32),
            pltpu.VMEM((len(REDUCE) * SH, NORB), F32),
            pltpu.VMEM((2 * SH, NORB), F32),
            pltpu.SemaphoreType.DMA((len(SEM),)),
            pltpu.SemaphoreType.DMA((len(SEM),)),
            pltpu.SemaphoreType.DMA((3,)),
        ],
        compiler_params=pltpu.CompilerParams(
            collective_id=0, has_side_effects=True, vmem_limit_bytes=67_043_328
        ),
    )(orbitals, kernel)


def solution(mesh):
    placed = (P("blk", None), P("blk", "split", None))
    return jax.shard_map(
        per_device, mesh=mesh, in_specs=placed, out_specs=P(("blk", "split"), None), check_vma=False
    )
```

```python
import jax
import jax.numpy as jnp
from jax import lax
from jax.experimental import pallas as pl
from jax.experimental.pallas import tpu as pltpu
from jax.sharding import PartitionSpec as P

MESH = pl.DeviceIdType.MESH
F32 = jnp.float32
BF16 = jnp.bfloat16

NX, NZ, NC = 2, 8, 2
NXL, NY = 2, 8
SH = 32
NORB = 512
PB = 512
GCH = 2
RCH = 2
GR = SH // GCH
RR = SH // RCH
WIDE = 2 * NC * SH
BATCH = 2 * WIDE


def longest(plane, sign):
    return 4 if sign == (1 if plane == 0 else -1) else 3


CHAINS = [(plane, sign) for plane in (0, 1) for sign in (1, -1)]
GATHER = [("gx", k) for k in range(GCH)] + [
    ("gz", plane, sign, hop, k)
    for plane, sign in CHAINS
    for hop in range(1, longest(plane, sign) + 1)
    for k in range(GCH)
]
NEAR, FAR = (0, 1, 7, 2, 6), (3, 5, 4)
CORE = [("gc", plane, off in NEAR) for plane in (0, 1) for off in (0, 4)]
REDUCE = [
    ("r", plane, sign, dist, k)
    for plane, sign in CHAINS
    for dist in range(1, longest(plane, sign) + 1)
    for k in range(RCH)
]
FOLD = [("rx", k) for k in range(RCH)]
SEM = {name: at for at, name in enumerate(GATHER + CORE + REDUCE + FOLD)}
SLOT = {name: at for at, name in enumerate(REDUCE)}
KINDS = {"gx": (0, SH), "gz": (1, len(GATHER) * GR - SH), "gc": (2, 2 * NZ * SH), "r": (3, len(REDUCE) * RR), "rx": (4, SH)}


def split_bf16(value):
    high = value.astype(BF16)
    return high, (value - high.astype(F32)).astype(BF16)


def rows_by_rows(a, b):
    return lax.dot_general(a, b, (((1,), (1,)), ((), ())), preferred_element_type=F32)


def rows_by_cols(a, b):
    return jnp.dot(a, b, preferred_element_type=F32)


def exchange(
    orb_hbm, ker_hbm, out_ref, ker, orb, gat, lhs, rhs, dens, wts, part, landed, folded, ssem, rsem, lsem
):
    b = lax.axis_index("blk")
    s = lax.axis_index("split")
    xh, z, c = b // (NZ * NC), (b // NC) % NZ, b % NC
    xl, y = s // NY, s % NY

    def blk_of(plane, off):
        return ((xh + plane) % NX) * (NZ * NC) + ((z + off + NZ) % NZ) * NC + c

    x_peer = (blk_of(1, 0), s)
    core_peer = (b + 1 - 2 * c, s)
    z_peer = {sign: (blk_of(0, sign), s) for sign in (1, -1)}
    y_peer = {sign: (b, xl * NY + (y + sign + NY) % NY) for sign in (1, -1)}
    xl_peer = (b, ((xl + 1) % NXL) * NY + y)
    peers = [x_peer, core_peer, z_peer[1], z_peer[-1], y_peer[1], y_peer[-1], xl_peer]

    barrier = pltpu.get_barrier_semaphore()
    for peer in peers:
        pl.semaphore_signal(barrier, inc=1, device_id=peer, device_id_type=MESH)

    def piece(block, k):
        return pl.ds(pl.multiple_of(block * SH + k * GR, 8), GR)

    orb_copy = pltpu.make_async_copy(orb_hbm, orb, lsem.at[0])
    ker_copy = pltpu.make_async_copy(ker_hbm.at[:, 0, :], ker, lsem.at[1])
    own_copy = pltpu.make_async_copy(
        orb_hbm.at[pl.ds(pl.multiple_of(s * SH, SH), SH)],
        gat.at[pl.ds(pl.multiple_of(b * SH, SH), SH)],
        lsem.at[2],
    )
    own_copy.start()
    orb_copy.start()
    ker_copy.start()

    pl.semaphore_wait(barrier, len(peers))

    def remote(name, src, dst, peer):
        return pltpu.make_async_remote_copy(
            src_ref=src,
            dst_ref=dst,
            send_sem=ssem.at[KINDS[name[0]][0]],
            recv_sem=rsem.at[SEM[name]],
            device_id=peer,
            device_id_type=MESH,
        )

    def send(name, src, dst, peer):
        remote(name, src, dst, peer).start()

    def send_own(name, k, peer):
        send(name, orb_hbm.at[piece(s, k)], gat.at[piece(b, k)], peer)

    def send_piece(name, block, k, peer):
        send(name, gat.at[piece(block, k)], gat.at[piece(block, k)], peer)

    def wait_piece(name, block, k, peer):
        remote(name, gat.at[piece(block, k)], gat.at[piece(block, k)], peer).wait_recv()

    for k in range(GCH):
        send_own(("gx", k), k, x_peer)
        for sign in (1, -1):
            send_own(("gz", 0, sign, 1, k), k, z_peer[sign])
    for k in range(GCH):
        send_own(("gc", 0, True), k, core_peer)

    orb_copy.wait()
    high, low = split_bf16(orb[...])
    lhs[:, pl.ds(0, NORB)] = high
    lhs[:, pl.ds(NORB, NORB)] = low

    def take_x(k):
        block = blk_of(1, 0)
        wait_piece(("gx", k), block, k, x_peer)
        for sign in (1, -1):
            send_piece(("gz", 1, sign, 1, k), block, k, z_peer[sign])
        send_piece(("gc", 1, True), block, k, core_peer)

    def take_hop(plane, hop, k):
        for sign in (1, -1):
            if hop > longest(plane, sign):
                continue
            block = blk_of(plane, -sign * hop)
            wait_piece(("gz", plane, sign, hop, k), block, k, z_peer[sign])
            if hop < longest(plane, sign):
                send_piece(("gz", plane, sign, hop + 1, k), block, k, z_peer[sign])
            send_piece(("gc", plane, hop <= 2), block, k, core_peer)

    def wait_core(plane, is_near):
        rows = pl.ds(0, len(NEAR if is_near else FAR) * SH)
        remote(("gc", plane, is_near), gat.at[rows], gat.at[rows], core_peer).wait_recv()

    half = NZ // 2
    pair0 = z // 2
    near = 2 * (z % 2) - 1
    pairs = {
        "near": [pair0, (pair0 + near + half) % half],
        "far": [(pair0 - near + half) % half, (pair0 + 2) % half],
    }

    def columns(plane, pair):
        at = ((xh + plane) % NX) * (NZ * NC * SH) + pair * WIDE
        return pl.ds(pl.multiple_of(at, WIDE), WIDE)

    def weigh(plane, which):
        for at, pair in enumerate(pairs[which]):
            high, low = split_bf16(gat[columns(plane, pair), :])
            rhs[pl.ds(at * WIDE, WIDE), pl.ds(0, NORB)] = high
            rhs[pl.ds(at * WIDE, WIDE), pl.ds(NORB, NORB)] = low
        g_high, g_low = rhs[:, pl.ds(0, NORB)], rhs[:, pl.ds(NORB, NORB)]
        for start in (0, PB // 2):
            rows = pl.ds(start, PB // 2)
            o_high, o_low = lhs[rows, pl.ds(0, NORB)], lhs[rows, pl.ds(NORB, NORB)]
            dens[rows, :] = (
                rows_by_rows(o_high, g_high) + rows_by_rows(o_low, g_high) + rows_by_rows(o_high, g_low)
            )
        for at, pair in enumerate(pairs[which]):
            weighted = dens[:, pl.ds(at * WIDE, WIDE)] * ker[:, columns(plane, pair)]
            high, low = split_bf16(weighted)
            wts[:, pl.ds(at * WIDE, WIDE)] = high
            wts[:, pl.ds(BATCH + at * WIDE, WIDE)] = low

    def apply(first):
        w_high, w_low = wts[:, pl.ds(0, BATCH)], wts[:, pl.ds(BATCH, BATCH)]
        for start in (0, NORB // 2):
            cols = pl.ds(start, NORB // 2)
            g_high, g_low = rhs[:, cols], rhs[:, pl.ds(NORB + start, NORB // 2)]
            product = (
                rows_by_cols(w_high, g_high) + rows_by_cols(w_low, g_high) + rows_by_cols(w_high, g_low)
            )
            part[:, cols] = product if first else part[:, cols] + product

    steps = []
    for k in range(GCH):
        steps.append((3.8 + 1.4 * k, lambda k=k: take_x(k)))
        for hop in range(1, 5):
            steps.append((2.4 * hop + 0.7 * k, lambda hop=hop, k=k: take_hop(0, hop, k)))
            steps.append((4.2 + 2.4 * hop + 0.7 * k, lambda hop=hop, k=k: take_hop(1, hop, k)))

    def near_own():
        ker_copy.wait()
        own_copy.wait()
        wait_core(0, True)
        weigh(0, "near")

    def near_other():
        wait_core(1, True)
        weigh(1, "near")

    def far_own():
        wait_core(0, False)
        weigh(0, "far")

    steps.append((6.3, near_own))
    steps.append((7.6, lambda: apply(True)))
    steps.append((10.6, near_other))
    steps.append((11.4, lambda: apply(False)))
    steps.append((12.2, far_own))
    steps.append((12.3, lambda: apply(False)))
    for _, step in sorted(steps, key=lambda entry: entry[0]):
        step()
    wait_core(1, False)
    weigh(1, "far")
    apply(False)

    def target(plane, off, k):
        share = ((xl + plane) % NXL) * NY + (y + off + NY) % NY
        return pl.ds(pl.multiple_of(share * SH + k * RR, 8), RR)

    def slot(name):
        return pl.ds(SLOT[name] * RR, RR)

    def send_partial(plane, sign, dist, k):
        name = ("r", plane, sign, dist, k)
        send(name, part.at[target(plane, sign * dist, k)], landed.at[slot(name)], y_peer[sign])

    def take_partial(plane, sign, dist, k):
        name = ("r", plane, sign, dist, k)
        remote(name, landed.at[slot(name)], landed.at[slot(name)], y_peer[sign]).wait_recv()
        return landed[slot(name), :]

    order = [(1, -1), (1, 1), (0, 1), (0, -1)]
    for step in range(4):
        for k in range(RCH):
            for plane, sign in order:
                dist = longest(plane, sign) - step
                if dist < 1:
                    continue
                if step:
                    part[target(plane, sign * dist, k), :] += take_partial(plane, sign, dist + 1, k)
                send_partial(plane, sign, dist, k)

    for k in range(RCH):
        here, there = pl.ds(k * RR, RR), pl.ds(SH + k * RR, RR)
        folded[here, :] = (
            part[target(1, 0, k), :] + take_partial(1, 1, 1, k) + take_partial(1, -1, 1, k)
        )
        send(("rx", k), folded.at[here], folded.at[there], xl_peer)
    for k in range(RCH):
        here, there = pl.ds(k * RR, RR), pl.ds(SH + k * RR, RR)
        mine = part[target(0, 0, k), :] + take_partial(0, 1, 1, k) + take_partial(0, -1, 1, k)
        remote(("rx", k), folded.at[here], folded.at[there], xl_peer).wait_recv()
        out_ref[here, :] = mine + folded[there, :]

    for name, peer in (("gx", 0), x_peer), (("gz", 0, 1, 1, 0), z_peer[1]), (("gc", 0, True), core_peer):
        rows = pl.ds(0, KINDS[name[0]][1])
        remote(name, gat.at[rows], gat.at[rows], peer).wait_send()
    rows = pl.ds(0, KINDS["r"][1])
    remote(("r", 0, 1, 1, 0), landed.at[rows], landed.at[rows], y_peer[1]).wait_send()
    rows = pl.ds(0, SH)
    remote(("rx", 0), folded.at[rows], folded.at[rows], xl_peer).wait_send()


def per_device(orbitals, kernel):
    columns = kernel.shape[2]
    return pl.pallas_call(
        exchange,
        out_shape=jax.ShapeDtypeStruct((SH, NORB), F32),
        in_specs=[pl.BlockSpec(memory_space=pltpu.HBM)] * 2,
        out_specs=pl.BlockSpec(memory_space=pltpu.VMEM),
        scratch_shapes=[
            pltpu.VMEM((PB, columns), F32),
            pltpu.VMEM((PB, NORB), F32),
            pltpu.VMEM((columns, NORB), F32),
            pltpu.VMEM((PB, 2 * NORB), BF16),
            pltpu.VMEM((BATCH, 2 * NORB), BF16),
            pltpu.VMEM((PB, BATCH), F32),
            pltpu.VMEM((PB, 2 * BATCH), BF16),
            pltpu.VMEM((PB, NORB), F32),
            pltpu.VMEM((len(REDUCE) * RR, NORB), F32),
            pltpu.VMEM((2 * SH, NORB), F32),
            pltpu.SemaphoreType.DMA((len(KINDS),)),
            pltpu.SemaphoreType.DMA((len(SEM),)),
            pltpu.SemaphoreType.DMA((3,)),
        ],
        compiler_params=pltpu.CompilerParams(
            collective_id=0, has_side_effects=True, vmem_limit_bytes=50_000_000
        ),
    )(*(pltpu.with_memory_space_constraint(array, pltpu.HBM) for array in (orbitals, kernel)))


def solution(mesh):
    placed = (P("blk", None), P("blk", "split", None))
    return jax.shard_map(
        per_device, mesh=mesh, in_specs=placed, out_specs=P(("blk", "split"), None), check_vma=False
    )
```

```python
import jax
import jax.numpy as jnp
from jax import lax
from jax.experimental import pallas as pl
from jax.experimental.pallas import tpu as pltpu
from jax.sharding import PartitionSpec as P

MESH = pl.DeviceIdType.MESH
F32 = jnp.float32
BF16 = jnp.bfloat16

NX, NZ, NC = 2, 8, 2
NXL, NY = 2, 8
SH = 32
NORB = 512
PB = 512
GCH = 2
RCH = 2
GR = SH // GCH
RR = SH // RCH
WIDE = 2 * NC * SH
BATCH = 2 * WIDE


HOPS = 4


def longest(plane, sign):
    return 4 if sign == (1 if plane == 0 else -1) else 3


CHAINS = [(plane, sign) for plane in (0, 1) for sign in (1, -1)]


def group_of(plane, hop):
    return ("a" if hop < HOPS else "b") if plane == 0 else ("b" if hop < 2 else "c")


GATHER = [("gx", k) for k in range(GCH)] + [
    ("gz", plane, hop, k) for plane in (0, 1) for hop in range(1, HOPS + 1) for k in range(GCH)
]
CORE = [("gc", name) for name in "abc"]
IN_GROUP = {
    name: sum(group_of(plane, hop) == name for plane in (0, 1) for hop in range(HOPS + 1)) for name in "abc"
}
REDUCE = [
    ("r", plane, sign, dist, k)
    for plane, sign in CHAINS
    for dist in range(1, longest(plane, sign) + 1)
    for k in range(RCH)
]
FOLD = [("rx", k) for k in range(RCH)]
BACK = [(plane, hop) for plane in (0, 1) for hop in (1, 2, 3)]
MERGE = {"ma": [(0, 1), (0, 2)], "mb": [(0, 3)], "mc": [(1, 1), (1, 2), (1, 3)]}
RETURN = [("ret", plane) for plane in (0, 1)]
SEM = {name: at for at, name in enumerate(GATHER + CORE + REDUCE + FOLD + [(name,) for name in MERGE] + RETURN)}
SLOT = {name: at for at, name in enumerate(REDUCE)}
KINDS = {
    "gx": (0, SH), "gz": (1, 2 * HOPS * SH), "gc": (2, 2 * (HOPS + 1) * SH), "r": (3, len(REDUCE) * RR), "rx": (4, SH),
    "ma": (5, 2 * SH), "mb": (6, SH), "mc": (7, 3 * SH), "ret": (8, len(BACK) * SH),
}


def split_bf16(value):
    high = value.astype(BF16)
    return high, (value - high.astype(F32)).astype(BF16)


def rows_by_rows(a, b):
    return lax.dot_general(a, b, (((1,), (1,)), ((), ())), preferred_element_type=F32)


def rows_by_cols(a, b):
    return jnp.dot(a, b, preferred_element_type=F32)


def exchange(
    orb_hbm, ker_hbm, out_ref,
    ker, orb, gat, lhs, rhs, dens, wts, turned, part, landed, folded, back, merged, returned, ssem, rsem, lsem
):
    b = lax.axis_index("blk")
    s = lax.axis_index("split")
    xh, z, c = b // (NZ * NC), (b // NC) % NZ, b % NC
    xl, y = s // NY, s % NY

    def blk_of(plane, off):
        return ((xh + plane) % NX) * (NZ * NC) + ((z + off + NZ) % NZ) * NC + c

    def source(plane, hop):
        return blk_of(plane, -hop if plane == 0 else hop)

    x_peer = (blk_of(1, 0), s)
    core_peer = (b + 1 - 2 * c, s)
    z_peer = [(blk_of(0, 1), s), (blk_of(0, -1), s)]
    y_peer = {sign: (b, xl * NY + (y + sign + NY) % NY) for sign in (1, -1)}
    xl_peer = (b, ((xl + 1) % NXL) * NY + y)
    peers = [x_peer, core_peer, y_peer[1], y_peer[-1], xl_peer]
    peers += [(blk_of(plane, off), s) for plane in (0, 1) for off in (1, -1, 2, -2, 3, -3)]

    barrier = pltpu.get_barrier_semaphore()
    for peer in peers:
        pl.semaphore_signal(barrier, inc=1, device_id=peer, device_id_type=MESH)

    def piece(block, k):
        return pl.ds(pl.multiple_of(block * SH + k * GR, 8), GR)

    def share(block):
        return pl.ds(pl.multiple_of(block * SH, SH), SH)

    orb_copy = pltpu.make_async_copy(orb_hbm, orb, lsem.at[0])
    ker_copy = pltpu.make_async_copy(ker_hbm.at[:, 0, :], ker, lsem.at[1])
    own_copy = pltpu.make_async_copy(orb_hbm.at[share(s)], gat.at[share(b)], lsem.at[2])
    own_copy.start()
    orb_copy.start()
    ker_copy.start()

    half = NZ // 2
    pair0 = z // 2

    def columns(plane, off):
        pair = (pair0 + off + half) % half
        at = ((xh + plane) % NX) * (NZ * NC * SH) + pair * WIDE
        return pl.ds(pl.multiple_of(at, WIDE), WIDE)

    for plane, off in ((0, 1), (1, 5)):
        chip = ((xh + plane) % NX) * NZ + (z + off + 2 * (z % 2)) % NZ
        gat[pl.ds(pl.multiple_of(chip * NC * SH, NC * SH), NC * SH), :] = jnp.zeros((NC * SH, NORB), F32)

    pl.semaphore_wait(barrier, len(peers))

    def remote(name, src, dst, peer):
        return pltpu.make_async_remote_copy(
            src_ref=src,
            dst_ref=dst,
            send_sem=ssem.at[KINDS[name[0]][0]],
            recv_sem=rsem.at[SEM[name]],
            device_id=peer,
            device_id_type=MESH,
        )

    def send(name, src, dst, peer):
        remote(name, src, dst, peer).start()

    def send_own(name, k, peer):
        send(name, orb_hbm.at[piece(s, k)], gat.at[piece(b, k)], peer)

    def send_piece(name, block, k, peer):
        send(name, gat.at[piece(block, k)], gat.at[piece(block, k)], peer)

    def wait_piece(name, block, k, peer):
        remote(name, gat.at[piece(block, k)], gat.at[piece(block, k)], peer).wait_recv()

    for k in range(GCH):
        send_own(("gx", k), k, x_peer)
        send_own(("gz", 0, 1, k), k, z_peer[0])
    for k in range(GCH):
        send_own(("gc", group_of(0, 0)), k, core_peer)

    orb_copy.wait()
    high, low = split_bf16(orb[...])
    lhs[:, pl.ds(0, NORB)] = high
    lhs[:, pl.ds(NORB, NORB)] = low

    def take_x(k):
        block = source(1, 0)
        wait_piece(("gx", k), block, k, x_peer)
        send_piece(("gz", 1, 1, k), block, k, z_peer[1])
        send_piece(("gc", group_of(1, 0)), block, k, core_peer)

    def take_hop(plane, hop, k):
        block = source(plane, hop)
        wait_piece(("gz", plane, hop, k), block, k, z_peer[plane])
        if hop < HOPS:
            send_piece(("gz", plane, hop + 1, k), block, k, z_peer[plane])
        send_piece(("gc", group_of(plane, hop)), block, k, core_peer)

    def wait_core(name):
        rows = pl.ds(0, IN_GROUP[name] * SH)
        remote(("gc", name), gat.at[rows], gat.at[rows], core_peer).wait_recv()

    batches = {
        "a": [columns(0, 0), columns(0, -1)],
        "b": [columns(0, -2), columns(1, 0)],
        "c": [columns(1, 1), columns(1, 2)],
    }

    def weigh(name):
        wait_core(name)
        for at, rows in enumerate(batches[name]):
            high, low = split_bf16(gat[rows, :])
            rhs[pl.ds(at * WIDE, WIDE), pl.ds(0, NORB)] = high
            rhs[pl.ds(at * WIDE, WIDE), pl.ds(NORB, NORB)] = low
        g_high, g_low = rhs[:, pl.ds(0, NORB)], rhs[:, pl.ds(NORB, NORB)]
        for start in (0, PB // 2):
            rows = pl.ds(start, PB // 2)
            o_high, o_low = lhs[rows, pl.ds(0, NORB)], lhs[rows, pl.ds(NORB, NORB)]
            dens[rows, :] = (
                rows_by_rows(o_high, g_high) + rows_by_rows(o_low, g_high) + rows_by_rows(o_high, g_low)
            )
        for at, cols in enumerate(batches[name]):
            high, low = split_bf16(dens[:, pl.ds(at * WIDE, WIDE)] * ker[:, cols])
            wts[:, pl.ds(at * WIDE, WIDE)] = high
            wts[:, pl.ds(BATCH + at * WIDE, WIDE)] = low

    def apply(first):
        w_high, w_low = wts[:, pl.ds(0, BATCH)], wts[:, pl.ds(BATCH, BATCH)]
        for start in (0, NORB // 2):
            cols = pl.ds(start, NORB // 2)
            g_high, g_low = rhs[:, cols], rhs[:, pl.ds(NORB + start, NORB // 2)]
            product = (
                rows_by_cols(w_high, g_high) + rows_by_cols(w_low, g_high) + rows_by_cols(w_high, g_low)
            )
            part[:, cols] = product if first else part[:, cols] + product

    def apply_back(name):
        for start in (0, PB // 2):
            rows = pl.ds(start, PB // 2)
            turned[:, pl.ds(start, PB // 2)] = wts[rows, pl.ds(0, BATCH)].T
            turned[:, pl.ds(PB + start, PB // 2)] = wts[rows, pl.ds(BATCH, BATCH)].T
        w_high, w_low = turned[:, pl.ds(0, PB)], turned[:, pl.ds(PB, PB)]
        for start in (0, NORB // 2):
            cols = pl.ds(start, NORB // 2)
            o_high, o_low = lhs[:, cols], lhs[:, pl.ds(NORB + start, NORB // 2)]
            product = (
                rows_by_cols(w_high, o_high) + rows_by_cols(w_low, o_high) + rows_by_cols(w_high, o_low)
            )
            for at, rows in enumerate(batches[name]):
                back[rows, cols] = product[at * WIDE : (at + 1) * WIDE, :]

    def merge_rows(plane, hop):
        return pl.ds(BACK.index((plane, hop)) * SH, SH)

    def send_merge(name):
        for plane, hop in MERGE[name]:
            block = source(plane, hop) + 1 - 2 * c
            send((name,), back.at[share(block)], merged.at[merge_rows(plane, hop)], core_peer)

    def merge(name):
        rows = pl.ds(0, len(MERGE[name]) * SH)
        remote((name,), back.at[rows], merged.at[rows], core_peer).wait_recv()
        for plane, hop in MERGE[name]:
            back[share(source(plane, hop)), :] += merged[merge_rows(plane, hop), :]

    def send_back(plane):
        for hop in (3, 2, 1):
            block = source(plane, hop)
            send(("ret", plane), back.at[share(block)], returned.at[merge_rows(plane, hop)], (block, s))

    steps = []
    for k in range(GCH):
        steps.append((3.8 + 1.0 * k, lambda k=k: take_x(k)))
        for hop in range(1, HOPS + 1):
            steps.append((2.5 * hop + 0.5 * k, lambda hop=hop, k=k: take_hop(0, hop, k)))
            steps.append((4.3 + 2.5 * hop + 0.5 * k, lambda hop=hop, k=k: take_hop(1, hop, k)))

    def first_weigh():
        ker_copy.wait()
        own_copy.wait()
        weigh("a")

    steps.append((10.61, first_weigh))
    steps.append((10.62, lambda: apply(True)))
    steps.append((11.9, lambda: apply_back("a")))
    steps.append((11.91, lambda: send_merge("ma")))
    steps.append((12.41, lambda: weigh("b")))
    steps.append((12.42, lambda: apply(False)))
    steps.append((12.43, lambda: apply_back("b")))
    steps.append((12.44, lambda: send_merge("mb")))
    for _, step in sorted(steps, key=lambda entry: entry[0]):
        step()
    weigh("c")
    apply(False)

    def target(plane, off, k):
        at = ((xl + plane) % NXL) * NY + (y + off + NY) % NY
        return pl.ds(pl.multiple_of(at * SH + k * RR, 8), RR)

    def slot(name):
        return pl.ds(SLOT[name] * RR, RR)

    def send_partial(plane, sign, dist, k):
        name = ("r", plane, sign, dist, k)
        send(name, part.at[target(plane, sign * dist, k)], landed.at[slot(name)], y_peer[sign])

    def take_partial(plane, sign, dist, k):
        name = ("r", plane, sign, dist, k)
        remote(name, landed.at[slot(name)], landed.at[slot(name)], y_peer[sign]).wait_recv()
        return landed[slot(name), :]

    def reduce_step(step):
        for k in range(RCH):
            for plane, sign in ((1, -1), (1, 1), (0, 1), (0, -1)):
                dist = longest(plane, sign) - step
                if dist < 1:
                    continue
                if step:
                    part[target(plane, sign * dist, k), :] += take_partial(plane, sign, dist + 1, k)
                send_partial(plane, sign, dist, k)

    reduce_step(0)
    apply_back("c")
    send_merge("mc")
    merge("ma")
    merge("mb")
    send_back(0)
    reduce_step(1)
    merge("mc")
    send_back(1)
    reduce_step(2)
    reduce_step(3)

    for k in range(RCH):
        here, there = pl.ds(k * RR, RR), pl.ds(SH + k * RR, RR)
        folded[here, :] = (
            part[target(1, 0, k), :] + take_partial(1, 1, 1, k) + take_partial(1, -1, 1, k)
        )
        send(("rx", k), folded.at[here], folded.at[there], xl_peer)
    for plane in (0, 1):
        rows = pl.ds(plane * 3 * SH, 3 * SH)
        remote(("ret", plane), returned.at[rows], returned.at[rows], z_peer[0]).wait_recv()
    for k in range(RCH):
        here, there = pl.ds(k * RR, RR), pl.ds(SH + k * RR, RR)
        mine = part[target(0, 0, k), :] + take_partial(0, 1, 1, k) + take_partial(0, -1, 1, k)
        for at in range(len(BACK)):
            mine += returned[pl.ds(at * SH + k * RR, RR), :]
        remote(("rx", k), folded.at[here], folded.at[there], xl_peer).wait_recv()
        out_ref[here, :] = mine + folded[there, :]

    for name, buffer in (
        (("gx", 0), gat), (("gz", 0, 1, 0), gat), (("gc", "a"), gat), (("r", 0, 1, 1, 0), landed), (("rx", 0), folded),
        (("ma",), back), (("mb",), back), (("mc",), back), (("ret", 0), back),
    ):
        rows = pl.ds(0, KINDS[name[0]][1])
        remote(name, buffer.at[rows], buffer.at[rows], core_peer).wait_send()


def per_device(orbitals, kernel):
    columns = kernel.shape[2]
    return pl.pallas_call(
        exchange,
        out_shape=jax.ShapeDtypeStruct((SH, NORB), F32),
        in_specs=[pl.BlockSpec(memory_space=pltpu.HBM)] * 2,
        out_specs=pl.BlockSpec(memory_space=pltpu.VMEM),
        scratch_shapes=[
            pltpu.VMEM((PB, columns), F32),
            pltpu.VMEM((PB, NORB), F32),
            pltpu.VMEM((columns, NORB), F32),
            pltpu.VMEM((PB, 2 * NORB), BF16),
            pltpu.VMEM((BATCH, 2 * NORB), BF16),
            pltpu.VMEM((PB, BATCH), F32),
            pltpu.VMEM((PB, 2 * BATCH), BF16),
            pltpu.VMEM((BATCH, 2 * PB), BF16),
            pltpu.VMEM((PB, NORB), F32),
            pltpu.VMEM((len(REDUCE) * RR, NORB), F32),
            pltpu.VMEM((2 * SH, NORB), F32),
            pltpu.VMEM((columns, NORB), F32),
            pltpu.VMEM((len(BACK) * SH, NORB), F32),
            pltpu.VMEM((len(BACK) * SH, NORB), F32),
            pltpu.SemaphoreType.DMA((len(KINDS),)),
            pltpu.SemaphoreType.DMA((len(SEM),)),
            pltpu.SemaphoreType.DMA((3,)),
        ],
        compiler_params=pltpu.CompilerParams(
            collective_id=0, has_side_effects=True, vmem_limit_bytes=50_000_000
        ),
    )(*(pltpu.with_memory_space_constraint(array, pltpu.HBM) for array in (orbitals, kernel)))


def solution(mesh):
    placed = (P("blk", None), P("blk", "split", None))
    return jax.shard_map(
        per_device, mesh=mesh, in_specs=placed, out_specs=P(("blk", "split"), None), check_vma=False
    )
```
